256 devices in a mesh: fn: 8 (over z_hi, core), pt: 32 (over x, y, z_lo).
Axes of the slice: x: 4, y: 4, z: 8 (z_hi: 4, z_lo: 2; z = z_hi * 2 + z_lo), core: 2. Of those that a mesh axis runs over, the one named last changes fastest.
Arguments:
- functions: bfloat16 [16384, 4096], P(('fn', 'pt')), may hold values from -6 to 6
- branch_in: bfloat16 [4096, 256], replicated, may hold values from -0.09375 to 0.09375
- branch_out: bfloat16 [256, 128], replicated, may hold values from -0.375 to 0.375
- branch_tangent: bfloat16 [256, 128], replicated, may hold values from -0.375 to 0.375
- points: float32 [2, 32768], P(None, ('pt', 'fn')), may hold values from 0 to 1
- trunk_in: float32 [2, 256], replicated, may hold values from -4 to 4
- trunk_bias: float32 [256], replicated, may hold values from -1 to 1
- trunk_out: bfloat16 [256, 128], replicated, may hold values from -0.375 to 0.375
- trunk_tangent: bfloat16 [256, 128], replicated, may hold values from -0.375 to 0.375
- slopes: bfloat16 [2, 16384, 32768], P(None, 'fn', 'pt'), may hold values from -4 to 4
Outputs:
- row_grad: float32 [16384, 128], P(('fn', 'pt'))
- branch_grad: float32 [256, 128], replicated
- trunk_grad: float32 [256, 128], replicated
The draws below stay inside these ranges and needn't reach their ends.
All inputs are finite; a program needn't handle non-finite values.
Results may differ from the reference program's by a relative error of at most 0.0041.
Values may be sent and summed in bfloat16 or wider, within the bound.
No kernel may reach another device: no remote copies, remote signals or barrier semaphores. Data moves between devices by JAX's collectives and lax.ppermute only.
A program may use at most 192 MiB of HBM per device.

```python
import math
import jax
import jax.numpy as jnp
from jax import lax

SENSORS = 4096
BRANCH_W = 256
TRUNK_W = 256
LATENT = 128
FUNCTIONS = 16384
POINTS = 32768


def steps_of(rng, extent, split, least, high):
    gain = 1.0
    for dim, shards_of in split:
        heights = jax.random.uniform(jax.random.fold_in(jax.random.fold_in(rng, 6), dim), (shards_of,), jnp.float32, least / len(split), high / len(split))
        gain = gain * jnp.repeat(jnp.exp(heights), extent[dim] // shards_of).reshape((-1,) + (1,) * (len(extent) - 1 - dim))
    return gain


def normal_values(rng, dims, width, reach, shards=(), held_as=jnp.bfloat16):
    gain = steps_of(rng, dims, shards, -0.22, 0.18) if shards else 1.0
    array = jax.random.normal(rng, dims, jnp.float32) * width * gain
    return jnp.minimum(jnp.maximum(array, -reach), reach).astype(held_as)


def setup_inputs(seed: int = 0) -> dict:
    key_of = jax.random.split(jax.random.key(seed), 11)
    functions = normal_values(key_of[0], (FUNCTIONS, SENSORS), 1.0, 6.0, ((0, 256),))
    branch_in = normal_values(key_of[1], (SENSORS, BRANCH_W), SENSORS ** -0.5, 0.09375)
    branch_out = normal_values(key_of[2], (BRANCH_W, LATENT), BRANCH_W ** -0.5, 0.375)
    branch_tangent = normal_values(key_of[3], (BRANCH_W, LATENT), BRANCH_W ** -0.5, 0.375)
    points = jnp.clip(1.0 * jax.random.uniform(key_of[4], (2, POINTS), jnp.float32) ** steps_of(key_of[4], (2, POINTS), ((1, 256),), -0.2, 0.2), 0.0, 1.0)
    trunk_in = normal_values(key_of[5], (2, TRUNK_W), 1.0, 4.0, (), jnp.float32)
    trunk_bias = jnp.clip(jax.random.uniform(key_of[6], (TRUNK_W,), jnp.float32, -1.0, 1.0), -1.0, 1.0)
    trunk_out = normal_values(key_of[7], (TRUNK_W, LATENT), TRUNK_W ** -0.5, 0.375)
    trunk_tangent = normal_values(key_of[8], (TRUNK_W, LATENT), TRUNK_W ** -0.5, 0.375)
    slopes = normal_values(key_of[9], (2, FUNCTIONS, POINTS), 1.0, 4.0, ((1, 8), (2, 32)))
    return dict(functions=functions, branch_in=branch_in, branch_out=branch_out, branch_tangent=branch_tangent, points=points, trunk_in=trunk_in, trunk_bias=trunk_bias, trunk_out=trunk_out, trunk_tangent=trunk_tangent, slopes=slopes)


def jet_features(points, trunk_in, trunk_bias):
    preact = points[0][:, None] * trunk_in[0][None, :] + points[1][:, None] * trunk_in[1][None, :] + trunk_bias[None, :]
    tanh_value = jnp.tanh(preact)
    first_deriv = 1.0 - tanh_value * tanh_value
    second_deriv = -2.0 * tanh_value * first_deriv
    square_sum = trunk_in[0] * trunk_in[0] + trunk_in[1] * trunk_in[1]
    return jnp.stack([second_deriv * square_sum[None, :], first_deriv * trunk_in[0][None, :], first_deriv * trunk_in[1][None, :]]).astype(jnp.bfloat16)


def reference(functions, branch_in, branch_out, branch_tangent, points, trunk_in, trunk_bias, trunk_out, trunk_tangent, slopes):
    highest = lax.Precision.HIGHEST
    hidden = jnp.tanh(jnp.dot(functions, branch_in, preferred_element_type=jnp.float32)).astype(jnp.bfloat16)
    latent = jnp.dot(hidden, branch_out, preferred_element_type=jnp.float32).astype(jnp.bfloat16)
    latent_tan = jnp.dot(hidden, branch_tangent, preferred_element_type=jnp.float32).astype(jnp.bfloat16)
    features = jet_features(points, trunk_in, trunk_bias)
    feat_wide = features.astype(jnp.float32)
    trunk_val = jnp.einsum("cjk,kp->cjp", feat_wide, trunk_out.astype(jnp.float32), precision=highest).astype(jnp.bfloat16)
    trunk_tan = jnp.einsum("cjk,kp->cjp", feat_wide, trunk_tangent.astype(jnp.float32), precision=highest).astype(jnp.bfloat16)
    point_factors = jnp.concatenate([trunk_tan, trunk_val], axis=2).astype(jnp.float32)
    trunk_wide = trunk_val.astype(jnp.float32)
    row_factors = jnp.concatenate([latent, latent_tan], axis=1).astype(jnp.float32)
    latent_wide = latent.astype(jnp.float32)
    block_size = math.gcd(FUNCTIONS, 512)
    block_count = FUNCTIONS // block_size

    def one_block(running, block_index):
        first_row = (block_index * block_size).astype(jnp.int32)
        row_block = lax.dynamic_slice_in_dim(row_factors, first_row, block_size, 0)
        latent_block = lax.dynamic_slice_in_dim(latent_wide, first_row, block_size, 0)
        slope_block = lax.dynamic_slice_in_dim(slopes, first_row, block_size, 1).astype(jnp.float32)
        response = jnp.einsum("ik,cjk->cij", row_block, point_factors, precision=highest)
        tangent = response[0] + slope_block[0] * response[1] + slope_block[1] * response[2]
        scaled = tangent * (1.0 / POINTS)
        weights = jnp.stack([scaled, slope_block[0] * scaled, slope_block[1] * scaled]).astype(jnp.bfloat16).astype(jnp.float32)
        row_part = jnp.einsum("cij,cjp->ip", weights, trunk_wide, precision=highest)
        running = running + jnp.einsum("cij,ip->jcp", weights, latent_block, precision=highest) * (1.0 / FUNCTIONS)
        return running, row_part

    start_grad = jnp.zeros((POINTS, 3, LATENT), jnp.float32)
    point_grad, row_parts = lax.scan(one_block, start_grad, jnp.arange(block_count, dtype=jnp.int32))
    row_grad = row_parts.reshape(FUNCTIONS, LATENT)
    branch_grad = jnp.dot(hidden.astype(jnp.float32).T, row_grad, precision=highest) * (1.0 / FUNCTIONS)
    trunk_grad = jnp.einsum("cjk,jcp->kp", feat_wide, point_grad, precision=highest)
    return row_grad, branch_grad, trunk_grad
```

```python
import functools

import jax
import jax.numpy as jnp
from jax import lax
from jax.experimental import pallas as pl
from jax.experimental.pallas import tpu as pltpu
from jax.sharding import PartitionSpec as P

F32 = jnp.float32
BF16 = jnp.bfloat16


def mm(a, b):
    return lax.dot_general(a, b, (((1,), (0,)), ((), ())), preferred_element_type=F32)


def mm_nt(a, b):
    return lax.dot_general(a, b, (((1,), (1,)), ((), ())), preferred_element_type=F32)


def mm_tn(a, b):
    return lax.dot_general(a, b, (((0,), (0,)), ((), ())), preferred_element_type=F32)


def trunk_kernel(points_ref, cols_ref, tangent_ref, out_ref, feat_ref, factor_ref):
    x, y = points_ref[0:1, :], points_ref[1:2, :]
    cx, cy, bias = cols_ref[:, 0:1], cols_ref[:, 1:2], cols_ref[:, 2:3]
    value = jnp.tanh(x * cx + y * cy + bias)
    first = 1.0 - value * value
    second = -2.0 * value * first
    feats = (second * (cx * cx + cy * cy), first * cx, first * cy)
    latent = out_ref.shape[1]
    for c in range(3):
        feat = feats[c].astype(BF16)
        feat_ref[c] = feat
        factor_ref[c, :latent, :] = mm_tn(tangent_ref[...], feat).astype(BF16)
        factor_ref[c, latent:, :] = mm_tn(out_ref[...], feat).astype(BF16)


def trunk(points, cols, trunk_tangent, trunk_out):
    width, latent = trunk_out.shape
    count = points.shape[1]
    tile = min(256, count)
    return pl.pallas_call(
        trunk_kernel,
        grid=(count // tile,),
        in_specs=[
            pl.BlockSpec((2, tile), lambda j: (0, j)),
            pl.BlockSpec((width, 3), lambda j: (0, 0)),
            pl.BlockSpec((width, latent), lambda j: (0, 0)),
            pl.BlockSpec((width, latent), lambda j: (0, 0)),
        ],
        out_specs=[
            pl.BlockSpec((3, width, tile), lambda j: (0, 0, j)),
            pl.BlockSpec((3, 2 * latent, tile), lambda j: (0, 0, j)),
        ],
        out_shape=[
            jax.ShapeDtypeStruct((3, width, count), BF16),
            jax.ShapeDtypeStruct((3, 2 * latent, count), BF16),
        ],
        cost_estimate=pl.CostEstimate(
            flops=12 * width * latent * count, bytes_accessed=12 * width * count, transcendentals=width * count
        ),
        name="trunk",
    )(points, cols, trunk_tangent, trunk_out)


def block_kernel(
    row_scale, grad_scale, col_tile, hidden_ref, slopes_ref, branch_out_ref, branch_tan_ref, factor_ref, feat_ref, out_ref, rows_ref, points_ref, branch_ref
):
    step, last = pl.program_id(0), pl.num_programs(0) - 1
    rows = hidden_ref.shape[0]
    latent = branch_out_ref.shape[1]
    count = factor_ref.shape[2]

    @pl.when(step == 0)
    def _():
        points_ref[...] = jnp.zeros_like(points_ref)
        branch_ref[...] = jnp.zeros_like(branch_ref)

    hidden = hidden_ref[...]
    lat = mm(hidden, branch_out_ref[...]).astype(BF16)
    row_factor = jnp.concatenate([lat, mm(hidden, branch_tan_ref[...]).astype(BF16)], axis=1)
    lat_t = lat.T
    total = jnp.zeros((rows, latent), F32)
    for j in range(0, count, col_tile):
        at = slice(j, j + col_tile)
        sx, sy = slopes_ref[0, :, at].astype(F32), slopes_ref[1, :, at].astype(F32)
        tangent = mm(row_factor, factor_ref[0, :, at])
        tangent = tangent + sx * mm(row_factor, factor_ref[1, :, at])
        tangent = tangent + sy * mm(row_factor, factor_ref[2, :, at])
        weights = (tangent.astype(BF16), (sx * tangent).astype(BF16), (sy * tangent).astype(BF16))
        for c in range(3):
            total = total + mm_nt(weights[c], factor_ref[c, latent:, at])
            points_ref[c, :, at] += mm(lat_t, weights[c])
    high = total.astype(BF16)
    low = (total - high.astype(F32)).astype(BF16)
    branch_ref[...] += mm_tn(hidden, high) + mm_tn(hidden, low)
    rows_ref[pl.ds(pl.multiple_of(step * rows, rows), rows), :] = (total * row_scale).astype(rows_ref.dtype)

    @pl.when(step == last)
    def _():
        members, height = out_ref.shape[0], out_ref.shape[1]
        own = rows_ref.shape[0] // members
        share = height - own
        trunk_grad = jnp.zeros((feat_ref.shape[1], latent), F32)
        for c in range(3):
            part = points_ref[c]
            high = part.astype(BF16)
            low = (part - high.astype(F32)).astype(BF16)
            trunk_grad = trunk_grad + mm_nt(feat_ref[c], high) + mm_nt(feat_ref[c], low)
        out_ref[:, :own, :] = rows_ref[...].reshape(members, own, latent)
        half = members // 2
        out_ref[:half, own:, :] = (branch_ref[...] * grad_scale).astype(out_ref.dtype).reshape(half, share, latent)
        out_ref[half:, own:, :] = (trunk_grad * grad_scale).astype(out_ref.dtype).reshape(half, share, latent)


def block(hidden, slopes, branch_out, branch_tangent, factor, feat, members, row_scale, grad_scale):
    rows, width = hidden.shape
    latent = branch_out.shape[1]
    count = slopes.shape[2]
    tile = min(256, rows)
    share = 2 * width // members
    resident = functools.partial(pl.BlockSpec, pipeline_mode=pl.Buffered(1))
    return pl.pallas_call(
        functools.partial(block_kernel, row_scale, grad_scale, min(256, count)),
        grid=(rows // tile,),
        in_specs=[
            pl.BlockSpec((tile, width), lambda i: (i, 0)),
            pl.BlockSpec((2, tile, count), lambda i: (0, i, 0)),
            resident((width, latent), lambda i: (0, 0)),
            resident((width, latent), lambda i: (0, 0)),
            resident((3, 2 * latent, count), lambda i: (0, 0, 0)),
            resident((3, feat.shape[1], count), lambda i: (0, 0, 0)),
        ],
        out_specs=pl.BlockSpec((members, rows // members + share, latent), lambda i: (0, 0, 0)),
        out_shape=jax.ShapeDtypeStruct((members, rows // members + share, latent), BF16),
        scratch_shapes=[
            pltpu.VMEM((rows, latent), BF16),
            pltpu.VMEM((3, latent, count), F32),
            pltpu.VMEM((width, latent), F32),
        ],
        cost_estimate=pl.CostEstimate(
            flops=2 * 3 * rows * count * 4 * latent, bytes_accessed=4 * rows * count, transcendentals=0
        ),
        compiler_params=pltpu.CompilerParams(vmem_limit_bytes=48 << 20),
        name="block",
    )(hidden, slopes, branch_out, branch_tangent, factor, feat)


def doubled(values, axis_name, combine):
    size = lax.axis_size(axis_name)
    me = lax.axis_index(axis_name)
    bit = 1
    while bit < size:
        other = lax.ppermute(values, axis_name, [(i, i ^ bit) for i in range(size)])
        values = combine(values, other, (me & bit) != 0)
        bit *= 2
    return values


def local(functions, branch_in, branch_out, branch_tangent, points, trunk_in, trunk_bias, trunk_out, trunk_tangent, slopes):
    members = lax.axis_size("pt")
    total_rows = functions.shape[0] * lax.axis_size("fn") * members
    total_points = points.shape[1] * lax.axis_size("fn") * members
    width = branch_in.shape[1]
    all_points = doubled(
        points,
        "fn",
        lambda mine, other, high: jnp.where(
            high, jnp.concatenate([other, mine], axis=1), jnp.concatenate([mine, other], axis=1)
        ),
    )
    hidden = jnp.tanh(jnp.dot(functions, branch_in, preferred_element_type=F32)).astype(BF16)
    own, latent = hidden.shape[0], branch_out.shape[1]
    hidden_all = lax.all_to_all(jnp.broadcast_to(hidden[None], (members,) + hidden.shape), "pt", 0, 0)
    hidden_all = hidden_all.reshape(members * own, width)
    cols = jnp.concatenate([trunk_in, trunk_bias[None]], axis=0).T
    feat, factor = trunk(all_points, cols, trunk_tangent, trunk_out)
    row_scale = 1.0 / total_points
    parts = block(
        hidden_all, slopes, branch_out, branch_tangent, factor, feat, members, row_scale, row_scale / total_rows
    )
    sums = jnp.sum(lax.all_to_all(parts, "pt", 0, 0).astype(F32), axis=0)
    row_grad = sums[:own]
    grads = doubled(sums[own:], "fn", lambda mine, other, high: mine + other)
    grads = lax.all_to_all(jnp.broadcast_to(grads[None], (members,) + grads.shape), "pt", 0, 0)
    grads = grads.reshape(2, width, latent)
    return (row_grad, grads[0], grads[1])


def solution(mesh):
    in_specs = (
        P(("fn", "pt"), None),
        P(),
        P(),
        P(),
        P(None, ("pt", "fn")),
        P(),
        P(),
        P(),
        P(),
        P(None, "fn", "pt"),
    )
    out_specs = (P(("fn", "pt"), None), P(), P())
    return jax.shard_map(local, mesh=mesh, in_specs=in_specs, out_specs=out_specs, check_vma=False)
```

```python
import functools

import jax
import jax.numpy as jnp
from jax import lax
from jax.experimental import pallas as pl
from jax.experimental.pallas import tpu as pltpu
from jax.sharding import PartitionSpec as P

F32 = jnp.float32
BF16 = jnp.bfloat16


def mm(a, b):
    return lax.dot_general(a, b, (((1,), (0,)), ((), ())), preferred_element_type=F32)


def mm_nt(a, b):
    return lax.dot_general(a, b, (((1,), (1,)), ((), ())), preferred_element_type=F32)


def mm_tn(a, b):
    return lax.dot_general(a, b, (((0,), (0,)), ((), ())), preferred_element_type=F32)


def trunk(points_ref, cols_ref, tangent_ref, out_ref, feat_ref, factor_ref, col_tile):
    cx, cy, bias = cols_ref[:, 0:1], cols_ref[:, 1:2], cols_ref[:, 2:3]
    square = cx * cx + cy * cy
    latent = out_ref.shape[1]
    for j in range(0, points_ref.shape[1], col_tile):
        at = slice(j, j + col_tile)
        value = jnp.tanh(points_ref[0:1, at] * cx + points_ref[1:2, at] * cy + bias)
        first = 1.0 - value * value
        second = -2.0 * value * first
        for c, feat in enumerate((second * square, first * cx, first * cy)):
            feat = feat.astype(BF16)
            feat_ref[c, :, at] = feat
            factor_ref[c, :latent, at] = mm_tn(tangent_ref[...], feat).astype(BF16)
            factor_ref[c, latent:, at] = mm_tn(out_ref[...], feat).astype(BF16)


def block_kernel(
    row_scale,
    grad_scale,
    col_tile,
    hidden_ref,
    slopes_ref,
    branch_out_ref,
    branch_tan_ref,
    at_ref,
    cols_ref,
    trunk_out_ref,
    trunk_tan_ref,
    out_ref,
    rows_ref,
    points_ref,
    branch_ref,
    feat_ref,
    factor_ref,
):
    step, last = pl.program_id(0), pl.num_programs(0) - 1
    rows = hidden_ref.shape[0]
    latent = branch_out_ref.shape[1]
    count = factor_ref.shape[2]

    @pl.when(step == 0)
    def _():
        points_ref[...] = jnp.zeros_like(points_ref)
        branch_ref[...] = jnp.zeros_like(branch_ref)
        trunk(at_ref, cols_ref, trunk_tan_ref, trunk_out_ref, feat_ref, factor_ref, col_tile)

    hidden = hidden_ref[...]
    lat = mm(hidden, branch_out_ref[...]).astype(BF16)
    row_factor = jnp.concatenate([lat, mm(hidden, branch_tan_ref[...]).astype(BF16)], axis=1)
    lat_t = lat.T
    total = jnp.zeros((rows, latent), F32)
    for j in range(0, count, col_tile):
        at = slice(j, j + col_tile)
        sx, sy = slopes_ref[0, :, at].astype(F32), slopes_ref[1, :, at].astype(F32)
        tangent = mm(row_factor, factor_ref[0, :, at])
        tangent = tangent + sx * mm(row_factor, factor_ref[1, :, at])
        tangent = tangent + sy * mm(row_factor, factor_ref[2, :, at])
        weights = (tangent.astype(BF16), (sx * tangent).astype(BF16), (sy * tangent).astype(BF16))
        for c in range(3):
            total = total + mm_nt(weights[c], factor_ref[c, latent:, at])
            points_ref[c, :, at] += mm(lat_t, weights[c])
    high = total.astype(BF16)
    low = (total - high.astype(F32)).astype(BF16)
    branch_ref[...] += mm_tn(hidden, high) + mm_tn(hidden, low)
    rows_ref[pl.ds(pl.multiple_of(step * rows, rows), rows), :] = (total * row_scale).astype(rows_ref.dtype)

    @pl.when(step == last)
    def _():
        members, height = out_ref.shape[0], out_ref.shape[1]
        own = rows_ref.shape[0] // members
        share = height - own
        trunk_grad = jnp.zeros((feat_ref.shape[1], latent), F32)
        for c in range(3):
            part = points_ref[c]
            high = part.astype(BF16)
            low = (part - high.astype(F32)).astype(BF16)
            trunk_grad = trunk_grad + mm_nt(feat_ref[c], high) + mm_nt(feat_ref[c], low)
        out_ref[:, :own, :] = rows_ref[...].reshape(members, own, latent)
        half = members // 2
        out_ref[:half, own:, :] = (branch_ref[...] * grad_scale).astype(out_ref.dtype).reshape(half, share, latent)
        out_ref[half:, own:, :] = (trunk_grad * grad_scale).astype(out_ref.dtype).reshape(half, share, latent)


def block(hidden, slopes, branch_out, branch_tangent, points, cols, trunk_out, trunk_tangent, members, row_scale, grad_scale):
    rows, width = hidden.shape
    latent = branch_out.shape[1]
    count = slopes.shape[2]
    tile = min(512, rows)
    share = 2 * width // members
    resident = functools.partial(pl.BlockSpec, pipeline_mode=pl.Buffered(1))
    return pl.pallas_call(
        functools.partial(block_kernel, row_scale, grad_scale, min(256, count)),
        grid=(rows // tile,),
        in_specs=[
            pl.BlockSpec((tile, width), lambda i: (i, 0)),
            pl.BlockSpec((2, tile, count), lambda i: (0, i, 0)),
            resident((width, latent), lambda i: (0, 0)),
            resident((width, latent), lambda i: (0, 0)),
            resident(points.shape, lambda i: (0, 0)),
            resident(cols.shape, lambda i: (0, 0)),
            resident(trunk_out.shape, lambda i: (0, 0)),
            resident(trunk_out.shape, lambda i: (0, 0)),
        ],
        out_specs=pl.BlockSpec((members, rows // members + share, latent), lambda i: (0, 0, 0)),
        out_shape=jax.ShapeDtypeStruct((members, rows // members + share, latent), BF16),
        scratch_shapes=[
            pltpu.VMEM((rows, latent), BF16),
            pltpu.VMEM((3, latent, count), F32),
            pltpu.VMEM((width, latent), F32),
            pltpu.VMEM((3, trunk_out.shape[0], count), BF16),
            pltpu.VMEM((3, 2 * latent, count), BF16),
        ],
        cost_estimate=pl.CostEstimate(
            flops=2 * 3 * rows * count * 4 * latent, bytes_accessed=4 * rows * count, transcendentals=0
        ),
        compiler_params=pltpu.CompilerParams(vmem_limit_bytes=48 << 20),
        name="block",
    )(hidden, slopes, branch_out, branch_tangent, points, cols, trunk_out, trunk_tangent)


def points_of(points, mask):
    return lax.ppermute(points, "fn", [(i, i ^ mask) for i in range(lax.axis_size("fn"))])


def joined(mine, other, high):
    return jnp.where(high != 0, jnp.concatenate([other, mine], axis=1), jnp.concatenate([mine, other], axis=1))


def summed(values):
    size = lax.axis_size("fn")
    values = values + lax.ppermute(values, "fn", [(i, i ^ 1) for i in range(size)])
    ahead = [(i, (i + 2) % size) for i in range(size)]
    behind = lax.ppermute(values, "fn", ahead)
    opposite = lax.ppermute(behind, "fn", ahead)
    front = lax.ppermute(values, "fn", [(b, a) for a, b in ahead])
    return (values + opposite) + (behind + front)


def local(functions, branch_in, branch_out, branch_tangent, points, trunk_in, trunk_bias, trunk_out, trunk_tangent, slopes):
    members = lax.axis_size("pt")
    total_rows = functions.shape[0] * lax.axis_size("fn") * members
    total_points = points.shape[1] * lax.axis_size("fn") * members
    width = branch_in.shape[1]
    column = lax.axis_index("fn")
    first = joined(points, points_of(points, 1), column & 1)
    hidden = jnp.tanh(jnp.dot(functions, branch_in, preferred_element_type=F32)).astype(BF16)
    second = joined(first, points_of(first, 2), column & 2)
    own, latent = hidden.shape[0], branch_out.shape[1]
    copies, second = lax.optimization_barrier((jnp.broadcast_to(hidden[None], (members,) + hidden.shape), second))
    hidden_all = lax.all_to_all(copies, "pt", 0, 0)
    hidden_all = hidden_all.reshape(members * own, width)
    all_points = joined(second, points_of(second, 4), column & 4)
    cols = jnp.concatenate([trunk_in, trunk_bias[None]], axis=0).T
    row_scale = 1.0 / total_points
    parts = block(
        hidden_all,
        slopes,
        branch_out,
        branch_tangent,
        all_points,
        cols,
        trunk_out,
        trunk_tangent,
        members,
        row_scale,
        row_scale / total_rows,
    )
    sums = jnp.sum(lax.all_to_all(parts, "pt", 0, 0).astype(F32), axis=0)
    row_grad = sums[:own]
    grads = summed(sums[own:])
    grads = lax.all_to_all(jnp.broadcast_to(grads[None], (members,) + grads.shape), "pt", 0, 0)
    grads = grads.reshape(2, width, latent)
    return (row_grad, grads[0], grads[1])


def solution(mesh):
    in_specs = (
        P(("fn", "pt"), None),
        P(),
        P(),
        P(),
        P(None, ("pt", "fn")),
        P(),
        P(),
        P(),
        P(),
        P(None, "fn", "pt"),
    )
    out_specs = (P(("fn", "pt"), None), P(), P())
    return jax.shard_map(local, mesh=mesh, in_specs=in_specs, out_specs=out_specs, check_vma=False)
```

```python
import functools

import jax
import jax.numpy as jnp
from jax import lax
from jax.experimental import pallas as pl
from jax.experimental.pallas import tpu as pltpu
from jax.sharding import PartitionSpec as P

F32 = jnp.float32
BF16 = jnp.bfloat16


def mm(a, b):
    return lax.dot_general(a, b, (((1,), (0,)), ((), ())), preferred_element_type=F32)


def mm_nt(a, b):
    return lax.dot_general(a, b, (((1,), (1,)), ((), ())), preferred_element_type=F32)


def mm_tn(a, b):
    return lax.dot_general(a, b, (((0,), (0,)), ((), ())), preferred_element_type=F32)


def halves(values, axis):
    high = values.astype(BF16)
    return jnp.concatenate([high, (values - high.astype(F32)).astype(BF16)], axis=axis)


def trunk(points_ref, cols_ref, weights_ref, feat_ref, factor_ref, col_tile):
    cx, cy, bias = cols_ref[:, 0:1], cols_ref[:, 1:2], cols_ref[:, 2:3]
    square = cx * cx + cy * cy
    for j in range(0, points_ref.shape[1], col_tile):
        at = slice(j, j + col_tile)
        value = jnp.tanh(points_ref[0:1, at] * cx + points_ref[1:2, at] * cy + bias)
        first = 1.0 - value * value
        second = -2.0 * value * first
        for c, feat in enumerate((second * square, first * cx, first * cy)):
            feat = feat.astype(BF16)
            feat_ref[c, :, at] = feat
            factor_ref[c, :, at] = mm_tn(weights_ref[...], feat).astype(BF16)


def block_kernel(
    row_scale,
    grad_scale,
    col_tile,
    hidden_ref,
    slopes_ref,
    row_weights_ref,
    at_ref,
    cols_ref,
    point_weights_ref,
    out_ref,
    rows_ref,
    trunk_ref,
    branch_ref,
    feat_ref,
    factor_ref,
):
    step, last = pl.program_id(0), pl.num_programs(0) - 1
    rows = hidden_ref.shape[0]
    latent = row_weights_ref.shape[1] // 2
    count = factor_ref.shape[2]

    @pl.when(step == 0)
    def _():
        trunk_ref[...] = jnp.zeros_like(trunk_ref)
        branch_ref[...] = jnp.zeros_like(branch_ref)
        trunk(at_ref, cols_ref, point_weights_ref, feat_ref, factor_ref, col_tile)

    hidden = hidden_ref[...]
    row_factor = mm(hidden, row_weights_ref[...]).astype(BF16)
    trunk_out = point_weights_ref[:, latent:]
    spread = jnp.zeros((rows, feat_ref.shape[1]), F32)
    for j in range(0, count, col_tile):
        at = slice(j, j + col_tile)
        sx, sy = slopes_ref[0, :, at].astype(F32), slopes_ref[1, :, at].astype(F32)
        tangent = mm(row_factor, factor_ref[0, :, at])
        tangent = tangent + sx * mm(row_factor, factor_ref[1, :, at])
        tangent = tangent + sy * mm(row_factor, factor_ref[2, :, at])
        weights = (tangent.astype(BF16), (sx * tangent).astype(BF16), (sy * tangent).astype(BF16))
        for c in range(3):
            spread = spread + mm_nt(weights[c], feat_ref[c, :, at])
    spread = halves(spread, 1)
    total = mm(spread, jnp.concatenate([trunk_out, trunk_out], axis=0))
    trunk_ref[...] += mm_tn(spread, row_factor[:, :latent])
    branch_ref[...] += mm_tn(hidden, halves(total, 1))
    rows_ref[pl.ds(pl.multiple_of(step * rows, rows), rows), :] = (total * row_scale).astype(rows_ref.dtype)

    @pl.when(step == last)
    def _():
        members, height = out_ref.shape[0], out_ref.shape[1]
        own = rows_ref.shape[0] // members
        share = height - own
        half = trunk_ref.shape[0] // 2
        trunk_grad = trunk_ref[:half, :] + trunk_ref[half:, :]
        branch_grad = branch_ref[:, :latent] + branch_ref[:, latent:]
        out_ref[:, :own, :] = rows_ref[...].reshape(members, own, latent)
        half = members // 2
        out_ref[:half, own:, :] = (branch_grad * grad_scale).astype(out_ref.dtype).reshape(half, share, latent)
        out_ref[half:, own:, :] = (trunk_grad * grad_scale).astype(out_ref.dtype).reshape(half, share, latent)


def block(hidden, slopes, row_weights, points, cols, point_weights, members, row_scale, grad_scale):
    rows, width = hidden.shape
    latent = row_weights.shape[1] // 2
    count = slopes.shape[2]
    tile, col_tile = min(1024, rows), min(256, count)
    share = 2 * width // members
    resident = functools.partial(pl.BlockSpec, pipeline_mode=pl.Buffered(1))
    return pl.pallas_call(
        functools.partial(block_kernel, row_scale, grad_scale, col_tile),
        grid=(rows // tile,),
        in_specs=[
            pl.BlockSpec((tile, width), lambda i: (i, 0)),
            pl.BlockSpec((2, tile, count), lambda i: (0, i, 0)),
            resident(row_weights.shape, lambda i: (0, 0)),
            resident(points.shape, lambda i: (0, 0)),
            resident(cols.shape, lambda i: (0, 0)),
            resident(point_weights.shape, lambda i: (0, 0)),
        ],
        out_specs=pl.BlockSpec((members, rows // members + share, latent), lambda i: (0, 0, 0)),
        out_shape=jax.ShapeDtypeStruct((members, rows // members + share, latent), BF16),
        scratch_shapes=[
            pltpu.VMEM((rows, latent), BF16),
            pltpu.VMEM((2 * point_weights.shape[0], latent), F32),
            pltpu.VMEM((width, 2 * latent), F32),
            pltpu.VMEM((3, point_weights.shape[0], count), BF16),
            pltpu.VMEM((3, 2 * latent, count), BF16),
        ],
        cost_estimate=pl.CostEstimate(
            flops=2 * 3 * rows * count * 4 * latent, bytes_accessed=4 * rows * count, transcendentals=0
        ),
        compiler_params=pltpu.CompilerParams(vmem_limit_bytes=48 << 20),
        name="block",
    )(hidden, slopes, row_weights, points, cols, point_weights)


def points_of(points, mask):
    return lax.ppermute(points, "fn", [(i, i ^ mask) for i in range(lax.axis_size("fn"))])


def joined(mine, other, high):
    return jnp.where(high != 0, jnp.concatenate([other, mine], axis=1), jnp.concatenate([mine, other], axis=1))


def summed(values):
    size = lax.axis_size("fn")
    values = values + lax.ppermute(values, "fn", [(i, i ^ 1) for i in range(size)])
    ahead = [(i, (i + 2) % size) for i in range(size)]
    behind = lax.ppermute(values, "fn", ahead)
    opposite = lax.ppermute(behind, "fn", ahead)
    front = lax.ppermute(values, "fn", [(b, a) for a, b in ahead])
    return (values + opposite) + (behind + front)


def local(functions, branch_in, branch_out, branch_tangent, points, trunk_in, trunk_bias, trunk_out, trunk_tangent, slopes):
    members = lax.axis_size("pt")
    total_rows = functions.shape[0] * lax.axis_size("fn") * members
    total_points = points.shape[1] * lax.axis_size("fn") * members
    width = branch_in.shape[1]
    column = lax.axis_index("fn")
    first = joined(points, points_of(points, 1), column & 1)
    hidden = jnp.tanh(jnp.dot(functions, branch_in, preferred_element_type=F32)).astype(BF16)
    other = points_of(first, 2)
    second = joined(first, other, column & 2)
    own, latent = hidden.shape[0], branch_out.shape[1]
    copies = jnp.broadcast_to(hidden[None], (members,) + hidden.shape)
    hidden_all = lax.all_to_all(copies, "pt", 0, 0)
    hidden_all = hidden_all.reshape(members * own, width)
    all_points = joined(second, points_of(second, 4), column & 4)
    cols = jnp.concatenate([trunk_in, trunk_bias[None]], axis=0).T
    row_scale = 1.0 / total_points
    parts = block(
        hidden_all,
        slopes,
        jnp.concatenate([branch_out, branch_tangent], axis=1),
        all_points,
        cols,
        jnp.concatenate([trunk_tangent, trunk_out], axis=1),
        members,
        row_scale,
        row_scale / total_rows,
    )
    sums = jnp.sum(lax.all_to_all(parts, "pt", 0, 0).astype(F32), axis=0)
    row_grad = sums[:own]
    grads, row_grad = lax.optimization_barrier((summed(sums[own:]), row_grad))
    grads = lax.all_to_all(jnp.broadcast_to(grads[None], (members,) + grads.shape), "pt", 0, 0)
    grads = grads.reshape(2, width, latent)
    return (row_grad, grads[0], grads[1])


def solution(mesh):
    in_specs = (
        P(("fn", "pt"), None),
        P(),
        P(),
        P(),
        P(None, ("pt", "fn")),
        P(),
        P(),
        P(),
        P(),
        P(None, "fn", "pt"),
    )
    out_specs = (P(("fn", "pt"), None), P(), P())
    return jax.shard_map(local, mesh=mesh, in_specs=in_specs, out_specs=out_specs, check_vma=False)
```
